512 devices in a mesh: ax: 8 (over z_hi, x), az: 64 (over z_lo, y, core).
Axes of the slice: x: 4, y: 8, z: 8 (z_hi: 2, z_lo: 4; z = z_hi * 4 + z_lo), core: 2. Of those that a mesh axis runs over, the one named last changes fastest.
Arguments:
- state: float32 [4, 32, 512, 2048], P(None, 'ax', 'az'), may hold values from -6 to 6
- rotor_offset: int32 [1], replicated, may hold values from 136 to 375
- rotor_fraction: float32 [1], replicated, may hold values from 0 to 1
Outputs:
- new_state: float32 [4, 32, 512, 2048], P(None, 'ax', 'az')
The draws below stay inside these ranges and needn't reach their ends.
All inputs are finite; a program needn't handle non-finite values.
Results may differ from the reference program's by a relative error of at most 0.00002.
Values sent between devices are 32-bit elements; how exact they have to be, the bound alone decides.
No kernel may reach another device: no remote copies, remote signals or barrier semaphores. Data moves between devices by JAX's collectives and lax.ppermute only.
A program may use at most 64 MiB of HBM per device.

```python
import jax
import jax.numpy as jnp
from jax import lax

NV = 4
TH = 8
R = 2048
NP = 32
NTH = 512


def shard_levels(rng, extent, pieces, least, high):
    def one(axis_at, blocks):
        heights = jax.random.uniform(jax.random.fold_in(jax.random.fold_in(rng, 6), axis_at), (blocks,), jnp.float32, least / len(pieces), high / len(pieces))
        return jnp.repeat(jnp.exp(heights), extent[axis_at] // blocks).reshape((-1,) + (1,) * (len(extent) - axis_at - 1))

    gain = one(*pieces[0])
    for cut in pieces[1:]:
        gain = gain * one(*cut)
    return gain


def noise(rng, dims, scale, bound, split=(), kind=jnp.bfloat16):
    factor_of = shard_levels(rng, dims, split, -0.22, 0.18) if split else 1.0
    result = jax.random.normal(rng, dims, jnp.float32) * scale * factor_of
    return jnp.minimum(jnp.maximum(result, -bound), bound).astype(kind)


def setup_inputs(seed: int = 0) -> dict:
    splits = jax.random.split(jax.random.key(seed), 4)
    return {
        "state": noise(splits[0], (NV, NP, NTH, R), 1.0, 6.0, ((1, 8), (2, 64)), jnp.float32),
        "rotor_offset": jax.random.randint(splits[1], (1,), NTH // 4 + TH, 3 * NTH // 4 - TH).astype(jnp.int32),
        "rotor_fraction": jnp.clip(jax.random.uniform(splits[2], (1,), jnp.float32, 0.0, 1.0), 0.0, 1.0),
    }


step_size = 0.2
base_viscosity = 0.05
eddy_coeff = 0.05

def tendency(field, up_p, dn_p, up_t, dn_t, up_r, dn_r):
    grad_p = (up_p - dn_p) * 0.5
    grad_t = (up_t - dn_t) * 0.5
    grad_r = (up_r - dn_r) * 0.5
    second = up_p - 2.0 * field + dn_p + (up_t - 2.0 * field + dn_t) + (up_r - 2.0 * field + dn_r)
    strain = lax.optimization_barrier(jnp.sum(grad_p[:3] * grad_p[:3], axis=0)) + lax.optimization_barrier(jnp.sum(grad_t[:3] * grad_t[:3], axis=0)) + lax.optimization_barrier(jnp.sum(grad_r[:3] * grad_r[:3], axis=0))
    viscous = base_viscosity + eddy_coeff * jnp.sqrt(strain)
    advect = field[0] * grad_p + field[1] * grad_t + field[2] * grad_r
    return viscous * second - advect

def radial_sides(field, ghost_rot, ghost_sta):
    inner = field.shape[3] // 2
    zero = jnp.zeros(field.shape[:3] + (1,), field.dtype)
    up_r = jnp.concatenate([field[..., 1:inner], ghost_rot[..., None], field[..., inner + 1:], zero], axis=3)
    dn_r = jnp.concatenate([zero, field[..., :inner - 1], ghost_sta[..., None], field[..., inner:-1]], axis=3)
    return (up_r, dn_r)

def evaluate(field, offset, fraction):
    inner = field.shape[3] // 2
    stator_layer = field[..., inner]
    rotor_layer = field[..., inner - 1]
    ghost_rot = (1.0 - fraction) * jnp.roll(stator_layer, -offset, axis=2) + fraction * jnp.roll(stator_layer, -offset - 1, axis=2)
    ghost_sta = fraction * jnp.roll(rotor_layer, offset + 1, axis=2) + (1.0 - fraction) * jnp.roll(rotor_layer, offset, axis=2)
    zplane = jnp.zeros((field.shape[0], 1) + field.shape[2:], field.dtype)
    up_p = jnp.concatenate([field[:, 1:], zplane], axis=1)
    dn_p = jnp.concatenate([zplane, field[:, :-1]], axis=1)
    up_t = jnp.roll(field, -1, axis=2)
    dn_t = jnp.roll(field, 1, axis=2)
    up_r, dn_r = radial_sides(field, ghost_rot, ghost_sta)
    return tendency(field, up_p, dn_p, up_t, dn_t, up_r, dn_r)

def reference(state, rotor_offset, rotor_fraction):
    offset = rotor_offset[0]
    fraction = rotor_fraction[0]
    section = state + step_size * evaluate(state, offset, fraction)
    return 0.5 * (state + (section + step_size * evaluate(section, offset, fraction)))
```

```python
import functools

import jax
import jax.numpy as jnp
from jax import lax
from jax.experimental import pallas as pl
from jax.experimental.pallas import tpu as pltpu
from jax.sharding import PartitionSpec as P

DT = 0.2
NU = 0.05
EDDY = 0.05
LANE = 128
ROWS = 8
CHUNK = 256

f32 = jnp.float32


def iota(shape, dim):
    return lax.broadcasted_iota(jnp.int32, shape, dim)


def vmem():
    return pl.BlockSpec(memory_space=pltpu.VMEM)


def smem():
    return pl.BlockSpec(memory_space=pltpu.SMEM)


def hbm():
    return pl.BlockSpec(memory_space=pl.ANY)


def shape(*dims):
    return jax.ShapeDtypeStruct(dims, f32)


def params(mib=48):
    return pltpu.CompilerParams(vmem_limit_bytes=mib << 20)


def cross_kernel(start_ref, state, out, sem):
    copy = pltpu.make_async_copy(state.at[:, pl.ds(start_ref[0], 2)], out, sem)
    copy.start()
    copy.wait()


def pack_kernel(state, up_msg, dn_msg, low, high, st, sems):
    load = pltpu.make_async_copy(state, st, sems.at[0])
    load.start()
    load.wait()
    copy_low = pltpu.make_async_copy(st.at[:, 0:2], low, sems.at[1])
    copy_high = pltpu.make_async_copy(st.at[:, 2:4], high, sems.at[2])
    copy_low.start()
    copy_high.start()
    comps, planes, cells, radial = st.shape
    inner = radial // 2
    for c in range(comps):
        for p in range(planes):
            up_msg[c, p : p + 1, :] = st[c, p, cells - 1 : cells, :]
            up_msg[c, planes + p : planes + p + 1, :] = st[c, p, cells - 2 : cells - 1, :]
            dn_msg[c, p : p + 1, :] = st[c, p, 0:1, :]
            dn_msg[c, planes + p : planes + p + 1, :] = st[c, p, 1:2, :]
    lane = iota((ROWS, LANE), 1)
    zero = jnp.zeros((ROWS, radial - comps * LANE), f32)
    up_msg[comps, :, comps * LANE :] = zero
    dn_msg[comps, :, comps * LANE :] = zero
    for c in range(comps):
        tile = jnp.zeros((ROWS, LANE), f32)
        for p in range(planes):
            below = st[c, p, :, inner - LANE : inner]
            above = st[c, p, :, inner : inner + LANE]
            for layer, (source, at) in enumerate(((below, LANE - 2), (below, LANE - 1), (above, 0), (above, 1))):
                to = layer * 8 + p + 1
                tile = jnp.where(lane == to, pltpu.roll(source, (to - at) % LANE, 1), tile)
        up_msg[comps, :, c * LANE : (c + 1) * LANE] = tile
        dn_msg[comps, :, c * LANE : (c + 1) * LANE] = tile
    copy_low.wait()
    copy_high.wait()


def window_kernel(turn_ref, s_raw, w_raw, left, right, to_next, to_prev, s_win, w_win):
    comps = s_win.shape[0]
    planes = 4
    turn = turn_ref[0]
    radial = left.shape[2]
    lane = iota((2 * ROWS, LANE), 1)
    zero = jnp.zeros((ROWS, LANE), f32)

    def window(raw, c, start):
        cells = [raw[:, (k * comps + c) * LANE : (k * comps + c + 1) * LANE] for k in range(3)]
        whole = jnp.concatenate(cells + [zero], axis=0)
        return pltpu.roll(whole, 4 * ROWS - start, 0)[: 2 * ROWS]

    for c in range(comps):
        sw = window(s_raw, c, 7 + turn)
        ww = window(w_raw, c, 6 - turn)
        s_win[c] = sw
        w_win[c] = ww
        both = jnp.where(lane >= 16, sw, ww)
        for k in range(2):
            at = radial + (2 * c + k) * LANE
            to_next[:, at : at + LANE] = both[k * ROWS : (k + 1) * ROWS]
            to_prev[:, at : at + LANE] = both[k * ROWS : (k + 1) * ROWS]
        to_next[2 * c : 2 * c + 1, :radial] = left[c, planes - 1 : planes, :]
        to_next[2 * c + 1 : 2 * c + 2, :radial] = right[c, planes - 1 : planes, :]
        to_prev[2 * c : 2 * c + 1, :radial] = left[c, 0:1, :]
        to_prev[2 * c + 1 : 2 * c + 2, :radial] = right[c, 0:1, :]


def advance(q, up_p, dn_p, up_t, dn_t, up_r, dn_r):
    n = len(q)
    gp = [up_p[c] - dn_p[c] for c in range(n)]
    gt = [up_t[c] - dn_t[c] for c in range(n)]
    gr = [up_r[c] - dn_r[c] for c in range(n)]
    strain = gp[0] * gp[0] + gt[0] * gt[0] + gr[0] * gr[0]
    for c in (1, 2):
        strain = strain + (gp[c] * gp[c] + gt[c] * gt[c] + gr[c] * gr[c])
    visc = DT * NU + (DT * EDDY) * jnp.sqrt(0.25 * strain)
    v = [(0.5 * DT) * q[c] for c in range(3)]
    result = []
    for c in range(n):
        second = (up_p[c] + dn_p[c]) + (up_t[c] + dn_t[c]) + (up_r[c] + dn_r[c]) - 6.0 * q[c]
        carried = v[0] * gp[c] + v[1] * gt[c] + v[2] * gr[c]
        result.append(q[c] + (visc * second - carried))
    return result


def step_kernel(
    info, frac, state, crossed, from_prev, from_next,
    left, right, up_msg, dn_msg, low_edge, high_edge, s_win, w_win, own,
    out,
    field, sect, edge, edge_sect, ghost1, ghost2, result, sems,
):
    comps, planes, cells, radial = result.shape
    inner = radial // 2
    position, last, half = info[0], info[1], info[2]
    f = frac[0]
    body = slice(LANE, LANE + radial)
    get_state = pltpu.make_async_copy(state, field.at[:, 2 : 2 + planes, :, body], sems.at[0])
    get_state.start()
    low_dst = field.at[:, 0:2, :, body]
    high_dst = field.at[:, 2 + planes : 4 + planes, :, body]

    @pl.when(position == half)
    def _():
        pltpu.make_async_copy(crossed, low_dst, sems.at[1]).start()

    @pl.when(position != half)
    def _():
        pltpu.make_async_copy(from_prev, low_dst, sems.at[1]).start()

    @pl.when(position == half - 1)
    def _():
        pltpu.make_async_copy(crossed, high_dst, sems.at[2]).start()

    @pl.when(position != half - 1)
    def _():
        pltpu.make_async_copy(from_next, high_dst, sems.at[2]).start()

    for ref in (field, sect):
        side = jnp.zeros(ref.shape[:3] + (LANE,), f32)
        ref[:, :, :, 0:LANE] = side
        ref[:, :, :, LANE + radial :] = side
    for ref in (edge, edge_sect):
        side = jnp.zeros(ref.shape[:2] + (LANE,), f32)
        ref[:, :, 0:LANE] = side
        ref[:, :, LANE + radial :] = side

    lane = iota((2 * ROWS, LANE), 1)
    lane8 = iota((ROWS, LANE), 1)
    row8 = iota((ROWS, LANE), 0)

    def lanes(x, by):
        return pltpu.roll(x, by % LANE, 1)

    def rows(x, by):
        return pltpu.roll(x, by % x.shape[0], 0)

    s2, s3, w1, w0, own_s, own_w = [], [], [], [], [], []
    for c in range(comps):
        at = [radial + (2 * c + k) * LANE for k in range(2)]
        low = jnp.concatenate([low_edge[:, a : a + LANE] for a in at], axis=0)
        high = jnp.concatenate([high_edge[:, a : a + LANE] for a in at], axis=0)
        low, high = lanes(low, -planes), lanes(high, planes)
        is_low, is_high = lane % 8 == 0, lane % 8 == planes + 1
        sw = jnp.where(is_low, low, jnp.where(is_high, high, s_win[c]))
        ww = jnp.where(is_low, low, jnp.where(is_high, high, w_win[c]))
        s2.append(lanes(sw, -16))
        s3.append(lanes(sw, -24))
        w1.append(lanes(ww, -8))
        w0.append(ww)
        mine = [own[:, (k * comps + c) * LANE : (k * comps + c + 1) * LANE] for k in range(3)]
        mine = jnp.concatenate(mine + [jnp.zeros((ROWS, LANE), f32)], axis=0)
        own_s.append(lanes(mine, -16))
        own_w.append(lanes(mine, -8))

    def blend_rot(x):
        return (1.0 - f) * x + f * rows(x, -1)

    def blend_sta(x):
        return f * x + (1.0 - f) * rows(x, -1)

    for kind, layer, blend in ((0, s2, blend_rot), (1, w1, blend_sta)):
        for c in range(comps):
            g = blend(layer[c])
            here = rows(g, -1)[:ROWS]
            for s in range(planes + 2):
                ghost1[kind, s, c] = jnp.broadcast_to(here[:, s : s + 1], (ROWS, LANE))
            first = jnp.broadcast_to(g[0:1, :], (ROWS, LANE))
            after = jnp.broadcast_to(g[cells + 1 : cells + 2, :], (ROWS, LANE))
            picked = jnp.where(row8 < planes, first, after)
            picked = jnp.where(lane8 == row8 % planes + 1, picked, 0.0)
            ghost1[kind, planes + 2, c] = jnp.broadcast_to(jnp.sum(picked, axis=1, keepdims=True), (ROWS, LANE))

    def far_section(q, up_r, dn_r):
        return advance(
            q,
            [lanes(x, -1) for x in q], [lanes(x, 1) for x in q],
            [rows(x, -1) for x in q], [rows(x, 1) for x in q],
            up_r, dn_r,
        )

    far_sta = [rows(blend_sta(x), -6)[: 2 * ROWS] for x in own_w]
    far_rot = [rows(blend_rot(x), -6)[: 2 * ROWS] for x in own_s]
    sec_s = far_section(s2, s3, far_sta)
    sec_w = far_section(w1, far_rot, w0)
    for kind, layer, blend in ((0, sec_s, blend_rot), (1, sec_w, blend_sta)):
        for c in range(comps):
            here = rows(blend(layer[c]), -1)[:ROWS]
            for p in range(planes):
                ghost2[kind, p, c] = jnp.broadcast_to(here[:, p + 1 : p + 2], (ROWS, LANE))

    row = iota((ROWS, CHUNK), 0)
    column = iota((ROWS, CHUNK), 1)
    wide = CHUNK // LANE

    def radial_pair(load, rot, sta, base):
        ahead = load(base + LANE, CHUNK + LANE)
        behind = load(base, CHUNK + LANE)
        up = pltpu.roll(ahead, CHUNK + LANE - 1, 1)[:, :CHUNK]
        dn = pltpu.roll(behind, 1, 1)[:, LANE:]
        up = jnp.where(column == inner - 1 - base, jnp.concatenate([rot] * wide, 1), up)
        dn = jnp.where(column == inner - base, jnp.concatenate([sta] * wide, 1), dn)
        return up, dn

    def azimuthal_pair(q, before, after):
        up = jnp.where(row == cells - 1, after, pltpu.roll(q, ROWS - 1, 0))
        dn = jnp.where(row == 0, before, pltpu.roll(q, 1, 0))
        return up, dn

    def span(base, width):
        return pl.ds(pl.multiple_of(base, LANE), width)

    get_state.wait()
    pltpu.make_async_copy(from_prev, low_dst, sems.at[1]).wait()
    pltpu.make_async_copy(from_next, high_dst, sems.at[2]).wait()

    def build_edge(k, carry):
        base = k * CHUNK
        at = span(base, CHUNK)
        for c in range(comps):
            tile = jnp.where(row < planes, left[c, :, at], pltpu.roll(right[c, :, at], planes, 0))
            edge[c, :, span(base + LANE, CHUNK)] = tile
        return carry

    lax.fori_loop(0, radial // CHUNK, build_edge, 0)

    def first(k, carry):
        base = k * CHUNK
        at, padded = span(base, CHUNK), span(base + LANE, CHUNK)
        for s in range(planes + 2):
            q, up_p, dn_p, up_t, dn_t, up_r, dn_r = [], [], [], [], [], [], []
            for c in range(comps):
                x = field[c, s + 1, :, padded]
                q.append(x)
                up_p.append(field[c, s + 2, :, padded])
                dn_p.append(field[c, s, :, padded])
                if s == 0:
                    before, after = low_edge[2 * c : 2 * c + 1, at], low_edge[2 * c + 1 : 2 * c + 2, at]
                elif s == planes + 1:
                    before, after = high_edge[2 * c : 2 * c + 1, at], high_edge[2 * c + 1 : 2 * c + 2, at]
                else:
                    before, after = left[c, s - 1 : s, at], right[c, s - 1 : s, at]
                u, d = azimuthal_pair(x, before, after)
                up_t.append(u)
                dn_t.append(d)
                u, d = radial_pair(
                    lambda b, w: field[c, s + 1, :, span(b, w)], ghost1[0, s, c], ghost1[1, s, c], base
                )
                up_r.append(u)
                dn_r.append(d)
            new = advance(q, up_p, dn_p, up_t, dn_t, up_r, dn_r)
            for c in range(comps):
                value = new[c]
                if s == 0:
                    value = jnp.where(position == 0, 0.0, value)
                elif s == planes + 1:
                    value = jnp.where(position == last, 0.0, value)
                sect[c, s, :, padded] = value
        q, up_p, dn_p, up_t, dn_t, up_r, dn_r = [], [], [], [], [], [], []
        for c in range(comps):
            x = edge[c, :, padded]
            q.append(x)
            u, d = pltpu.roll(x, ROWS - 1, 0), pltpu.roll(x, 1, 0)
            u = jnp.where(row == planes - 1, high_edge[2 * c : 2 * c + 1, at], u)
            u = jnp.where(row == 2 * planes - 1, high_edge[2 * c + 1 : 2 * c + 2, at], u)
            d = jnp.where(row == 0, low_edge[2 * c : 2 * c + 1, at], d)
            d = jnp.where(row == planes, low_edge[2 * c + 1 : 2 * c + 2, at], d)
            up_p.append(u)
            dn_p.append(d)
            up_t.append(jnp.where(row < planes, dn_msg[c, :, at], right[c, :, at]))
            dn_t.append(pltpu.roll(jnp.where(row < planes, up_msg[c, :, at], left[c, :, at]), planes, 0))
            u, d = radial_pair(
                lambda b, w: edge[c, :, span(b, w)], ghost1[0, planes + 2, c], ghost1[1, planes + 2, c], base
            )
            up_r.append(u)
            dn_r.append(d)
        new = advance(q, up_p, dn_p, up_t, dn_t, up_r, dn_r)
        for c in range(comps):
            edge_sect[c, :, at] = new[c]
        return carry

    lax.fori_loop(0, radial // CHUNK, first, 0)

    def second(k, carry):
        base = k * CHUNK
        at, padded = span(base, CHUNK), span(base + LANE, CHUNK)
        for p in range(planes):
            q, up_p, dn_p, up_t, dn_t, up_r, dn_r = [], [], [], [], [], [], []
            for c in range(comps):
                x = sect[c, p + 1, :, padded]
                q.append(x)
                up_p.append(sect[c, p + 2, :, padded])
                dn_p.append(sect[c, p, :, padded])
                u, d = azimuthal_pair(x, edge_sect[c, p : p + 1, at], edge_sect[c, planes + p : planes + p + 1, at])
                up_t.append(u)
                dn_t.append(d)
                u, d = radial_pair(
                    lambda b, w: sect[c, p + 1, :, span(b, w)], ghost2[0, p, c], ghost2[1, p, c], base
                )
                up_r.append(u)
                dn_r.append(d)
            new = advance(q, up_p, dn_p, up_t, dn_t, up_r, dn_r)
            for c in range(comps):
                result[c, p, :, at] = 0.5 * (field[c, p + 2, :, padded] + new[c])
        return carry

    lax.fori_loop(0, radial // CHUNK, second, 0)
    put = pltpu.make_async_copy(result, out, sems.at[3])
    put.start()
    put.wait()


def shards(state, rotor_offset, rotor_fraction):
    comps, planes, cells, radial = state.shape
    n_ax, n_az = lax.axis_size("ax"), lax.axis_size("az")
    half = n_ax // 2
    position = lax.axis_index("ax")
    offset = rotor_offset[0]
    shift = (offset + cells // 2) // cells
    turn = (offset - shift * cells)[None]
    info = jnp.stack([position, jnp.int32(n_ax - 1), jnp.int32(half)])
    two = (comps, 2, cells, radial)
    dma = pltpu.SemaphoreType.DMA

    bulk = pl.pallas_call(
        cross_kernel,
        out_shape=shape(*two),
        in_specs=[smem(), hbm()],
        out_specs=hbm(),
        scratch_shapes=[dma],
        name="pack_cross",
    )(jnp.where(position < half, planes - 2, 0)[None], state)
    crossed = lax.ppermute(bulk, "ax", [(half - 1, half), (half, half - 1)])

    up_msg, dn_msg, low, high = pl.pallas_call(
        pack_kernel,
        out_shape=[shape(comps + 1, cells, radial)] * 2 + [shape(*two)] * 2,
        in_specs=[hbm()],
        out_specs=[vmem(), vmem(), hbm(), hbm()],
        scratch_shapes=[pltpu.VMEM(state.shape, f32), dma((3,))],
        compiler_params=params(16),
        name="pack",
    )(state)
    left = lax.ppermute(up_msg, "az", [(i, (i + 1) % n_az) for i in range(n_az)])
    right = lax.ppermute(dn_msg, "az", [((i + 1) % n_az, i) for i in range(n_az)])
    plain = [i for i in range(n_ax - 1) if i != half - 1]
    from_prev = lax.ppermute(high, "ax", [(i, i + 1) for i in plain])
    from_next = lax.ppermute(low, "ax", [(i + 1, i) for i in plain])

    own = jnp.concatenate([m[comps, :, : comps * LANE] for m in (left, up_msg, right)], axis=1)
    total = cells * n_az
    lowest = (total // 4 + 8 + cells // 2) // cells
    highest = (3 * total // 4 - 9 + cells // 2) // cells

    def moved(block, by):
        ahead = lax.ppermute(block, "az", [((i + by) % n_az, i) for i in range(n_az)])
        back = lax.ppermute(block, "az", [(i, (i + by) % n_az) for i in range(n_az)])
        return ahead, back

    s_raw, w_raw = lax.switch(
        shift - lowest, [functools.partial(moved, by=by) for by in range(lowest, highest + 1)], own
    )
    to_next, to_prev, s_win, w_win = pl.pallas_call(
        window_kernel,
        out_shape=[shape(cells, radial + 2 * comps * LANE)] * 2 + [shape(comps, 2 * cells, LANE)] * 2,
        in_specs=[smem()] + [vmem()] * 4,
        out_specs=[vmem()] * 4,
        compiler_params=params(16),
        name="pack_window",
    )(turn, s_raw, w_raw, left, right)
    low_edge = lax.ppermute(to_next, "ax", [(i, i + 1) for i in range(n_ax - 1)])
    high_edge = lax.ppermute(to_prev, "ax", [(i + 1, i) for i in range(n_ax - 1)])

    wide = radial + 2 * LANE
    return pl.pallas_call(
        step_kernel,
        out_shape=shape(*state.shape),
        in_specs=[smem(), smem()] + [hbm()] * 4 + [vmem()] * 9,
        out_specs=hbm(),
        scratch_shapes=[
            pltpu.VMEM((comps, planes + 4, cells, wide), f32),
            pltpu.VMEM((comps, planes + 2, cells, wide), f32),
            pltpu.VMEM((comps, 2 * planes, wide), f32),
            pltpu.VMEM((comps, 2 * planes, wide), f32),
            pltpu.VMEM((2, planes + 3, comps, ROWS, LANE), f32),
            pltpu.VMEM((2, planes, comps, ROWS, LANE), f32),
            pltpu.VMEM(state.shape, f32),
            dma((4,)),
        ],
        compiler_params=params(),
        name="step",
    )(
        info, rotor_fraction, state, crossed, from_prev, from_next,
        left, right, up_msg, dn_msg, low_edge, high_edge, s_win, w_win, own,
    )


def solution(mesh):
    return jax.shard_map(
        shards,
        mesh=mesh,
        in_specs=(P(None, "ax", "az", None), P(), P()),
        out_specs=P(None, "ax", "az", None),
        check_vma=False,
    )
```

```python
import jax
import jax.numpy as jnp
from jax import lax
from jax.experimental import pallas as pl
from jax.experimental.pallas import tpu as pltpu
from jax.sharding import PartitionSpec as P

DT = 0.2
NU = 0.05
EDDY = 0.05
LANE = 128
ROWS = 8
CHUNK = 256

f32 = jnp.float32


def iota(shape, dim):
    return lax.broadcasted_iota(jnp.int32, shape, dim)


def vmem():
    return pl.BlockSpec(memory_space=pltpu.VMEM)


def smem():
    return pl.BlockSpec(memory_space=pltpu.SMEM)


def hbm():
    return pl.BlockSpec(memory_space=pl.ANY)


def shape(*dims):
    return jax.ShapeDtypeStruct(dims, f32)


def params(mib=48):
    return pltpu.CompilerParams(vmem_limit_bytes=mib << 20)


def pack_kernel(st, up_msg, dn_msg, low, high, layers):
    comps, planes, cells, radial = st.shape
    inner = radial // 2
    lane = iota((ROWS, LANE), 1)
    tile = jnp.zeros((ROWS, LANE), f32)
    for c in range(comps):
        for p in range(planes):
            up_msg[c, p : p + 1, :] = st[c, p, cells - 1 : cells, :]
            up_msg[c, planes + p : planes + p + 1, :] = st[c, p, cells - 2 : cells - 1, :]
            dn_msg[c, p : p + 1, :] = st[c, p, 0:1, :]
            dn_msg[c, planes + p : planes + p + 1, :] = st[c, p, 1:2, :]
            below = st[c, p, :, inner - LANE : inner]
            above = st[c, p, :, inner : inner + LANE]
            for layer, (source, at) in enumerate(((below, LANE - 2), (below, LANE - 1), (above, 0), (above, 1))):
                to = layer * 32 + c * 8 + p + 1
                tile = jnp.where(lane == to, pltpu.roll(source, (to - at) % LANE, 1), tile)
        for k in range(2):
            low[c, k] = st[c, k]
            high[c, k] = st[c, planes - 2 + k]
    layers[...] = tile


def window_kernel(where_ref, tiles, left, right, to_next, to_prev, s_win, w_win, own):
    comps = left.shape[0]
    planes = left.shape[1] // 2
    radial = left.shape[2]
    count = tiles.shape[0]
    sector, shift, turn = where_ref[0], where_ref[1], where_ref[2]

    def around(centre):
        found = [tiles[lax.rem(centre + (count + k), count)] for k in (-1, 0, 1)]
        return jnp.concatenate(found + [jnp.zeros((ROWS, LANE), f32)], axis=0)

    def window(centre, start):
        return pltpu.roll(around(centre), 4 * ROWS - start, 0)[: 2 * ROWS]

    sw = window(sector + shift, 7 + turn)
    ww = window(sector + count - shift, 6 - turn)
    s_win[...] = sw
    w_win[...] = ww
    own[...] = around(sector)
    both = jnp.where(iota((2 * ROWS, LANE), 1) >= 64, sw, ww)
    for msg, plane in ((to_next, planes - 1), (to_prev, 0)):
        for k in range(2):
            msg[:, radial + k * LANE : radial + (k + 1) * LANE] = both[k * ROWS : (k + 1) * ROWS]
        for c in range(comps):
            msg[2 * c : 2 * c + 1, :radial] = left[c, plane : plane + 1, :]
            msg[2 * c + 1 : 2 * c + 2, :radial] = right[c, plane : plane + 1, :]


def advance(q, up_p, dn_p, up_t, dn_t, up_r, dn_r):
    n = len(q)
    gp = [up_p[c] - dn_p[c] for c in range(n)]
    gt = [up_t[c] - dn_t[c] for c in range(n)]
    gr = [up_r[c] - dn_r[c] for c in range(n)]
    strain = gp[0] * gp[0] + gt[0] * gt[0] + gr[0] * gr[0]
    for c in (1, 2):
        strain = strain + (gp[c] * gp[c] + gt[c] * gt[c] + gr[c] * gr[c])
    visc = DT * NU + (DT * EDDY) * jnp.sqrt(0.25 * strain)
    v = [(0.5 * DT) * q[c] for c in range(3)]
    result = []
    for c in range(n):
        second = (up_p[c] + dn_p[c]) + (up_t[c] + dn_t[c]) + (up_r[c] + dn_r[c]) - 6.0 * q[c]
        carried = v[0] * gp[c] + v[1] * gt[c] + v[2] * gr[c]
        result.append(q[c] + (visc * second - carried))
    return result


def lanes(x, by):
    return pltpu.roll(x, by % LANE, 1)


def rows(x, by):
    return pltpu.roll(x, by % x.shape[0], 0)


def blend_rot(x, f):
    return (1.0 - f) * x + f * rows(x, -1)


def blend_sta(x, f):
    return f * x + (1.0 - f) * rows(x, -1)


def spread(x, at):
    return jnp.broadcast_to(x[:ROWS, at : at + 1], (ROWS, LANE))


def span(base, width):
    return pl.ds(pl.multiple_of(base, LANE), width)


def radial_pair(load, rot, sta, base, inner):
    column = iota((ROWS, CHUNK), 1)
    wide = CHUNK // LANE
    up = pltpu.roll(load(base + LANE, CHUNK + LANE), CHUNK + LANE - 1, 1)[:, :CHUNK]
    dn = pltpu.roll(load(base, CHUNK + LANE), 1, 1)[:, LANE:]
    up = jnp.where(column == inner - 1 - base, jnp.concatenate([rot] * wide, 1), up)
    dn = jnp.where(column == inner - base, jnp.concatenate([sta] * wide, 1), dn)
    return up, dn


def azimuthal_pair(q, before, after):
    row = iota(q.shape, 0)
    up = jnp.where(row == ROWS - 1, after, pltpu.roll(q, ROWS - 1, 0))
    dn = jnp.where(row == 0, before, pltpu.roll(q, 1, 0))
    return up, dn


def pad_zero(ref):
    side = jnp.zeros(ref.shape[:-1] + (LANE,), f32)
    ref[..., :LANE] = side
    ref[..., ref.shape[-1] - LANE :] = side


def own_kernel(frac, st, near_low, near_high, left, right, s_win, w_win, sect, field, ghost):
    comps, planes, cells, radial = st.shape
    inner = radial // 2
    f = frac[0]
    pad_zero(field)
    pad_zero(sect)
    for kind, win, at, blend in ((0, s_win, 64, blend_rot), (1, w_win, 32, blend_sta)):
        here = rows(blend(win[...], f), -1)
        for c in range(comps):
            for p in range(planes):
                ghost[kind, p, c] = spread(here, at + 8 * c + p + 1)

    def copy(k, carry):
        base = k * CHUNK
        for c in range(comps):
            for p in range(planes):
                field[c, p, :, span(base + LANE, CHUNK)] = st[c, p, :, span(base, CHUNK)]
        return carry

    lax.fori_loop(0, radial // CHUNK, copy, 0)

    def body(k, carry):
        base = k * CHUNK
        at, padded = span(base, CHUNK), span(base + LANE, CHUNK)
        for p in range(planes):
            q, up_p, dn_p, up_t, dn_t, up_r, dn_r = [], [], [], [], [], [], []
            for c in range(comps):
                x = st[c, p, :, at]
                q.append(x)
                up_p.append(near_high[c, 0, :, at] if p == planes - 1 else st[c, p + 1, :, at])
                dn_p.append(near_low[c, 1, :, at] if p == 0 else st[c, p - 1, :, at])
                u, d = azimuthal_pair(x, left[c, p : p + 1, at], right[c, p : p + 1, at])
                up_t.append(u)
                dn_t.append(d)
                u, d = radial_pair(
                    lambda b, w: field[c, p, :, span(b, w)], ghost[0, p, c], ghost[1, p, c], base, inner
                )
                up_r.append(u)
                dn_r.append(d)
            new = advance(q, up_p, dn_p, up_t, dn_t, up_r, dn_r)
            for c in range(comps):
                sect[c, p, :, padded] = new[c]
        return carry

    lax.fori_loop(0, radial // CHUNK, body, 0)


def step_kernel(
    info, frac, st, near_low, near_high, sect, left, right, up_msg, dn_msg, late_low, late_high, s_win, w_win, own,
    out,
    near, near_sect, edge, edge_sect, ghost1, ghost2, result, sem,
):
    comps, planes, cells, radial = st.shape
    inner = radial // 2
    position, last = info[0], info[1]
    f = frac[0]
    for ref in (near, near_sect, edge):
        pad_zero(ref)

    lane = iota((2 * ROWS, LANE), 1)
    lane8 = iota((ROWS, LANE), 1)
    row8 = iota((ROWS, LANE), 0)
    s2, s3, w1, w0, own_s, own_w = [], [], [], [], [], []
    is_low, is_high = lane % 8 == 0, lane % 8 == planes + 1
    at = [radial + k * LANE for k in range(2)]
    low = jnp.concatenate([late_low[:, a : a + LANE] for a in at], axis=0)
    high = jnp.concatenate([late_high[:, a : a + LANE] for a in at], axis=0)
    low, high = lanes(low, -planes), lanes(high, planes)
    sw = jnp.where(is_low, low, jnp.where(is_high, high, s_win[...]))
    ww = jnp.where(is_low, low, jnp.where(is_high, high, w_win[...]))
    mine = own[...]
    for c in range(comps):
        s2.append(lanes(sw, -64 - 8 * c))
        s3.append(lanes(sw, -96 - 8 * c))
        w1.append(lanes(ww, -32 - 8 * c))
        w0.append(lanes(ww, -8 * c))
        own_s.append(lanes(mine, -64 - 8 * c))
        own_w.append(lanes(mine, -32 - 8 * c))

    for kind, layer, blend in ((0, s2, blend_rot), (1, w1, blend_sta)):
        for c in range(comps):
            g = blend(layer[c], f)
            here = rows(g, -1)
            ghost1[kind, 0, c] = spread(here, 0)
            ghost1[kind, 1, c] = spread(here, planes + 1)
            first = jnp.broadcast_to(g[0:1, :], (ROWS, LANE))
            after = jnp.broadcast_to(g[cells + 1 : cells + 2, :], (ROWS, LANE))
            picked = jnp.where(row8 < planes, first, after)
            picked = jnp.where(lane8 == row8 % planes + 1, picked, 0.0)
            ghost1[kind, 2, c] = jnp.broadcast_to(jnp.sum(picked, axis=1, keepdims=True), (ROWS, LANE))

    def far_section(q, up_r, dn_r):
        return advance(
            q,
            [lanes(x, -1) for x in q], [lanes(x, 1) for x in q],
            [rows(x, -1) for x in q], [rows(x, 1) for x in q],
            up_r, dn_r,
        )

    far_sta = [rows(blend_sta(x, f), -6)[: 2 * ROWS] for x in own_w]
    far_rot = [rows(blend_rot(x, f), -6)[: 2 * ROWS] for x in own_s]
    sec_s = far_section(s2, s3, far_sta)
    sec_w = far_section(w1, far_rot, w0)
    for kind, layer, blend in ((0, sec_s, blend_rot), (1, sec_w, blend_sta)):
        for c in range(comps):
            here = rows(blend(layer[c], f), -1)
            for p in range(planes):
                ghost2[kind, p, c] = spread(here, p + 1)

    row = iota((ROWS, CHUNK), 0)

    def build(k, carry):
        base = k * CHUNK
        at, padded = span(base, CHUNK), span(base + LANE, CHUNK)
        for c in range(comps):
            edge[c, :, padded] = jnp.where(row < planes, left[c, :, at], pltpu.roll(right[c, :, at], planes, 0))
            near[c, 0, :, padded] = near_low[c, 1, :, at]
            near[c, 1, :, padded] = near_high[c, 0, :, at]
        return carry

    lax.fori_loop(0, radial // CHUNK, build, 0)

    def first(k, carry):
        base = k * CHUNK
        at, padded = span(base, CHUNK), span(base + LANE, CHUNK)
        for s, late, outside in ((0, late_low, 0), (1, late_high, last)):
            q, up_p, dn_p, up_t, dn_t, up_r, dn_r = [], [], [], [], [], [], []
            for c in range(comps):
                x = near[c, s, :, padded]
                q.append(x)
                far = near_high[c, 1, :, at] if s else near_low[c, 0, :, at]
                up_p.append(far if s else st[c, 0, :, at])
                dn_p.append(st[c, planes - 1, :, at] if s else far)
                u, d = azimuthal_pair(x, late[2 * c : 2 * c + 1, at], late[2 * c + 1 : 2 * c + 2, at])
                up_t.append(u)
                dn_t.append(d)
                u, d = radial_pair(
                    lambda b, w: near[c, s, :, span(b, w)], ghost1[0, s, c], ghost1[1, s, c], base, inner
                )
                up_r.append(u)
                dn_r.append(d)
            new = advance(q, up_p, dn_p, up_t, dn_t, up_r, dn_r)
            for c in range(comps):
                near_sect[c, s, :, padded] = jnp.where(position == outside, 0.0, new[c])
        q, up_p, dn_p, up_t, dn_t, up_r, dn_r = [], [], [], [], [], [], []
        for c in range(comps):
            x = edge[c, :, padded]
            q.append(x)
            u, d = pltpu.roll(x, ROWS - 1, 0), pltpu.roll(x, 1, 0)
            u = jnp.where(row == planes - 1, late_high[2 * c : 2 * c + 1, at], u)
            u = jnp.where(row == 2 * planes - 1, late_high[2 * c + 1 : 2 * c + 2, at], u)
            d = jnp.where(row == 0, late_low[2 * c : 2 * c + 1, at], d)
            d = jnp.where(row == planes, late_low[2 * c + 1 : 2 * c + 2, at], d)
            up_p.append(u)
            dn_p.append(d)
            up_t.append(jnp.where(row < planes, dn_msg[c, :, at], right[c, :, at]))
            dn_t.append(pltpu.roll(jnp.where(row < planes, up_msg[c, :, at], left[c, :, at]), planes, 0))
            u, d = radial_pair(
                lambda b, w: edge[c, :, span(b, w)], ghost1[0, 2, c], ghost1[1, 2, c], base, inner
            )
            up_r.append(u)
            dn_r.append(d)
        new = advance(q, up_p, dn_p, up_t, dn_t, up_r, dn_r)
        for c in range(comps):
            edge_sect[c, :, at] = new[c]
        return carry

    lax.fori_loop(0, radial // CHUNK, first, 0)

    def second(k, carry):
        base = k * CHUNK
        at, padded = span(base, CHUNK), span(base + LANE, CHUNK)
        for p in range(planes):
            q, up_p, dn_p, up_t, dn_t, up_r, dn_r = [], [], [], [], [], [], []
            for c in range(comps):
                x = sect[c, p, :, padded]
                q.append(x)
                up_p.append(near_sect[c, 1, :, padded] if p == planes - 1 else sect[c, p + 1, :, padded])
                dn_p.append(near_sect[c, 0, :, padded] if p == 0 else sect[c, p - 1, :, padded])
                u, d = azimuthal_pair(x, edge_sect[c, p : p + 1, at], edge_sect[c, planes + p : planes + p + 1, at])
                up_t.append(u)
                dn_t.append(d)
                u, d = radial_pair(
                    lambda b, w: sect[c, p, :, span(b, w)], ghost2[0, p, c], ghost2[1, p, c], base, inner
                )
                up_r.append(u)
                dn_r.append(d)
            new = advance(q, up_p, dn_p, up_t, dn_t, up_r, dn_r)
            for c in range(comps):
                result[c, p, :, at] = 0.5 * (st[c, p, :, at] + new[c])
        pltpu.make_async_copy(result.at[:, :, :, at], out.at[:, :, :, at], sem).start()
        return carry

    lax.fori_loop(0, radial // CHUNK, second, 0)
    pltpu.make_async_copy(result, out, sem).wait()


def shards(state, rotor_offset, rotor_fraction):
    comps, planes, cells, radial = state.shape
    n_ax, n_az = lax.axis_size("ax"), lax.axis_size("az")
    position = lax.axis_index("ax")
    offset = rotor_offset[0]
    shift = (offset + cells // 2) // cells
    turn = offset - shift * cells
    where = jnp.stack([lax.axis_index("az"), shift, turn])
    info = jnp.stack([position, jnp.int32(n_ax - 1)])

    up_msg, dn_msg, low, high, layers = pl.pallas_call(
        pack_kernel,
        out_shape=[shape(comps, cells, radial)] * 2 + [shape(comps, 2, cells, radial)] * 2 + [shape(ROWS, LANE)],
        in_specs=[vmem()],
        out_specs=[vmem()] * 5,
        compiler_params=params(16),
        name="pack",
    )(state)
    onward = [(i, i + 1) for i in range(n_ax - 1)]
    backward = [(i + 1, i) for i in range(n_ax - 1)]
    from_prev = lax.ppermute(high, "ax", onward)
    from_next = lax.ppermute(low, "ax", backward)
    left = lax.ppermute(up_msg, "az", [(i, (i + 1) % n_az) for i in range(n_az)])
    right = lax.ppermute(dn_msg, "az", [((i + 1) % n_az, i) for i in range(n_az)])

    tiles = lax.all_to_all(jnp.broadcast_to(layers, (n_az, ROWS, LANE)), "az", 0, 0)
    to_next, to_prev, s_win, w_win, own = pl.pallas_call(
        window_kernel,
        out_shape=[shape(cells, radial + 2 * LANE)] * 2 + [shape(2 * cells, LANE)] * 2 + [shape(4 * cells, LANE)],
        in_specs=[smem()] + [vmem()] * 3,
        out_specs=[vmem()] * 5,
        compiler_params=params(16),
        name="pack_window",
    )(where, tiles, left, right)
    late_low = lax.ppermute(to_next, "ax", onward)
    late_high = lax.ppermute(to_prev, "ax", backward)

    wide = radial + 2 * LANE
    cells_all = planes * cells * radial
    sect = pl.pallas_call(
        own_kernel,
        out_shape=shape(comps, planes, cells, wide),
        in_specs=[smem()] + [vmem()] * 7,
        out_specs=vmem(),
        scratch_shapes=[
            pltpu.VMEM((comps, planes, cells, wide), f32),
            pltpu.VMEM((2, planes, comps, ROWS, LANE), f32),
        ],
        cost_estimate=pl.CostEstimate(flops=120 * cells_all, bytes_accessed=48 * cells_all, transcendentals=cells_all),
        compiler_params=params(16),
        name="own_section",
    )(rotor_fraction, state, from_prev, from_next, left, right, s_win, w_win)
    return pl.pallas_call(
        step_kernel,
        out_shape=shape(*state.shape),
        in_specs=[smem(), smem()] + [vmem()] * 13,
        out_specs=hbm(),
        scratch_shapes=[
            pltpu.VMEM((comps, 2, cells, wide), f32),
            pltpu.VMEM((comps, 2, cells, wide), f32),
            pltpu.VMEM((comps, 2 * planes, wide), f32),
            pltpu.VMEM((comps, 2 * planes, radial), f32),
            pltpu.VMEM((2, 3, comps, ROWS, LANE), f32),
            pltpu.VMEM((2, planes, comps, ROWS, LANE), f32),
            pltpu.VMEM(state.shape, f32),
            pltpu.SemaphoreType.DMA,
        ],
        compiler_params=params(24),
        name="step",
    )(
        info, rotor_fraction, state, from_prev, from_next, sect,
        left, right, up_msg, dn_msg, late_low, late_high, s_win, w_win, own,
    )


def solution(mesh):
    return jax.shard_map(
        shards,
        mesh=mesh,
        in_specs=(P(None, "ax", "az", None), P(), P()),
        out_specs=P(None, "ax", "az", None),
        check_vma=False,
    )
```

```python
import jax
import jax.numpy as jnp
from jax import lax
from jax.experimental import pallas as pl
from jax.experimental.pallas import tpu as pltpu
from jax.sharding import PartitionSpec as P

DT = 0.2
NU = 0.05
EDDY = 0.05
LANE = 128
ROWS = 8
CHUNK = 256

f32 = jnp.float32


def iota(shape, dim):
    return lax.broadcasted_iota(jnp.int32, shape, dim)


def vmem():
    return pl.BlockSpec(memory_space=pltpu.VMEM)


def smem():
    return pl.BlockSpec(memory_space=pltpu.SMEM)


def hbm():
    return pl.BlockSpec(memory_space=pl.ANY)


def shape(*dims):
    return jax.ShapeDtypeStruct(dims, f32)


def params(mib=48):
    return pltpu.CompilerParams(vmem_limit_bytes=mib << 20)


def cross_kernel(info, st, crossing):
    planes = st.shape[1]
    below = info[0] < info[2]
    for c in range(st.shape[0]):
        for k in range(2):
            crossing[c, k] = jnp.where(below, st[c, planes - 2 + k], st[c, k])


def pack_kernel(st, crossing, up_msg, dn_msg, low, high, layers):
    comps, planes, cells, radial = st.shape
    inner = radial // 2
    lane = iota((ROWS, LANE), 1)
    tile = jnp.zeros((ROWS, LANE), f32)
    for c in range(comps):
        for p in range(planes):
            up_msg[c, p : p + 1, :] = st[c, p, cells - 1 : cells, :]
            up_msg[c, planes + p : planes + p + 1, :] = st[c, p, cells - 2 : cells - 1, :]
            dn_msg[c, p : p + 1, :] = st[c, p, 0:1, :]
            dn_msg[c, planes + p : planes + p + 1, :] = st[c, p, 1:2, :]
            below = st[c, p, :, inner - LANE : inner]
            above = st[c, p, :, inner : inner + LANE]
            for layer, (source, at) in enumerate(((below, LANE - 2), (below, LANE - 1), (above, 0), (above, 1))):
                to = layer * 32 + c * 8 + p + 1
                tile = jnp.where(lane == to, pltpu.roll(source, (to - at) % LANE, 1), tile)
        for k in range(2):
            low[c, k] = st[c, k]
            high[c, k] = st[c, planes - 2 + k]
    layers[...] = tile


def window_kernel(where_ref, tiles, left, right, to_next, to_prev, s_win, w_win, own):
    comps = left.shape[0]
    planes = left.shape[1] // 2
    radial = left.shape[2]
    count = tiles.shape[0]
    sector, shift, turn = where_ref[0], where_ref[1], where_ref[2]

    def around(centre):
        found = [tiles[lax.rem(centre + (count + k), count)] for k in (-1, 0, 1)]
        return jnp.concatenate(found + [jnp.zeros((ROWS, LANE), f32)], axis=0)

    def window(centre, start):
        return pltpu.roll(around(centre), 4 * ROWS - start, 0)[: 2 * ROWS]

    sw = window(sector + shift, 7 + turn)
    ww = window(sector + count - shift, 6 - turn)
    s_win[...] = sw
    w_win[...] = ww
    own[...] = around(sector)
    both = jnp.where(iota((2 * ROWS, LANE), 1) >= 64, sw, ww)
    for msg, plane in ((to_next, planes - 1), (to_prev, 0)):
        for k in range(2):
            msg[:, radial + k * LANE : radial + (k + 1) * LANE] = both[k * ROWS : (k + 1) * ROWS]
        for c in range(comps):
            msg[2 * c : 2 * c + 1, :radial] = left[c, plane : plane + 1, :]
            msg[2 * c + 1 : 2 * c + 2, :radial] = right[c, plane : plane + 1, :]


def advance(q, up_p, dn_p, up_t, dn_t, up_r, dn_r):
    n = len(q)
    gp = [up_p[c] - dn_p[c] for c in range(n)]
    gt = [up_t[c] - dn_t[c] for c in range(n)]
    gr = [up_r[c] - dn_r[c] for c in range(n)]
    strain = gp[0] * gp[0] + gt[0] * gt[0] + gr[0] * gr[0]
    for c in (1, 2):
        strain = strain + (gp[c] * gp[c] + gt[c] * gt[c] + gr[c] * gr[c])
    visc = DT * NU + (DT * EDDY) * jnp.sqrt(0.25 * strain)
    v = [(0.5 * DT) * q[c] for c in range(3)]
    result = []
    for c in range(n):
        second = (up_p[c] + dn_p[c]) + (up_t[c] + dn_t[c]) + (up_r[c] + dn_r[c]) - 6.0 * q[c]
        carried = v[0] * gp[c] + v[1] * gt[c] + v[2] * gr[c]
        result.append(q[c] + (visc * second - carried))
    return result


def lanes(x, by):
    return pltpu.roll(x, by % LANE, 1)


def rows(x, by):
    return pltpu.roll(x, by % x.shape[0], 0)


def blend_rot(x, f):
    return (1.0 - f) * x + f * rows(x, -1)


def blend_sta(x, f):
    return f * x + (1.0 - f) * rows(x, -1)


def spread(x, at):
    return jnp.broadcast_to(x[:ROWS, at : at + 1], (ROWS, LANE))


def span(base, width):
    return pl.ds(pl.multiple_of(base, LANE), width)


def radial_pair(load, rot, sta, base, inner):
    column = iota((ROWS, CHUNK), 1)
    wide = CHUNK // LANE
    up = pltpu.roll(load(base + LANE, CHUNK + LANE), CHUNK + LANE - 1, 1)[:, :CHUNK]
    dn = pltpu.roll(load(base, CHUNK + LANE), 1, 1)[:, LANE:]
    up = jnp.where(column == inner - 1 - base, jnp.concatenate([rot] * wide, 1), up)
    dn = jnp.where(column == inner - base, jnp.concatenate([sta] * wide, 1), dn)
    return up, dn


def azimuthal_pair(q, before, after):
    row = iota(q.shape, 0)
    up = jnp.where(row == ROWS - 1, after, pltpu.roll(q, ROWS - 1, 0))
    dn = jnp.where(row == 0, before, pltpu.roll(q, 1, 0))
    return up, dn


def pad_zero(ref):
    side = jnp.zeros(ref.shape[:-1] + (LANE,), f32)
    ref[..., :LANE] = side
    ref[..., ref.shape[-1] - LANE :] = side


def choose(crossing, crossed, plain, c, k, at):
    return jnp.where(crossing, crossed[c, k, :, at], plain[c, k, :, at])


def own_kernel(info, frac, st, crossed, near_low, near_high, left, right, s_win, w_win, sect, field, ghost):
    comps, planes, cells, radial = st.shape
    inner = radial // 2
    f = frac[0]
    from_below, from_above = info[0] == info[2], info[0] == info[2] - 1
    pad_zero(field)
    pad_zero(sect)
    for kind, win, at, blend in ((0, s_win, 64, blend_rot), (1, w_win, 32, blend_sta)):
        here = rows(blend(win[...], f), -1)
        for c in range(comps):
            for p in range(planes):
                ghost[kind, p, c] = spread(here, at + 8 * c + p + 1)

    def copy(k, carry):
        base = k * CHUNK
        for c in range(comps):
            for p in range(planes):
                field[c, p, :, span(base + LANE, CHUNK)] = st[c, p, :, span(base, CHUNK)]
        return carry

    lax.fori_loop(0, radial // CHUNK, copy, 0)

    def body(k, carry):
        base = k * CHUNK
        at, padded = span(base, CHUNK), span(base + LANE, CHUNK)
        for p in range(planes):
            q, up_p, dn_p, up_t, dn_t, up_r, dn_r = [], [], [], [], [], [], []
            for c in range(comps):
                x = st[c, p, :, at]
                q.append(x)
                up_p.append(choose(from_above, crossed, near_high, c, 0, at) if p == planes - 1 else st[c, p + 1, :, at])
                dn_p.append(choose(from_below, crossed, near_low, c, 1, at) if p == 0 else st[c, p - 1, :, at])
                u, d = azimuthal_pair(x, left[c, p : p + 1, at], right[c, p : p + 1, at])
                up_t.append(u)
                dn_t.append(d)
                u, d = radial_pair(
                    lambda b, w: field[c, p, :, span(b, w)], ghost[0, p, c], ghost[1, p, c], base, inner
                )
                up_r.append(u)
                dn_r.append(d)
            new = advance(q, up_p, dn_p, up_t, dn_t, up_r, dn_r)
            for c in range(comps):
                sect[c, p, :, padded] = new[c]
        return carry

    lax.fori_loop(0, radial // CHUNK, body, 0)


def step_kernel(
    info, frac, st, crossed, near_low, near_high, sect, left, right, up_msg, dn_msg, late_low, late_high, s_win, w_win, own,
    out,
    near, near_sect, edge, edge_sect, ghost1, ghost2, result, sem,
):
    comps, planes, cells, radial = st.shape
    inner = radial // 2
    position, last = info[0], info[1]
    from_below, from_above = position == info[2], position == info[2] - 1
    f = frac[0]
    for ref in (near, near_sect, edge):
        pad_zero(ref)

    lane = iota((2 * ROWS, LANE), 1)
    lane8 = iota((ROWS, LANE), 1)
    row8 = iota((ROWS, LANE), 0)
    s2, s3, w1, w0, own_s, own_w = [], [], [], [], [], []
    is_low, is_high = lane % 8 == 0, lane % 8 == planes + 1
    at = [radial + k * LANE for k in range(2)]
    low = jnp.concatenate([late_low[:, a : a + LANE] for a in at], axis=0)
    high = jnp.concatenate([late_high[:, a : a + LANE] for a in at], axis=0)
    low, high = lanes(low, -planes), lanes(high, planes)
    sw = jnp.where(is_low, low, jnp.where(is_high, high, s_win[...]))
    ww = jnp.where(is_low, low, jnp.where(is_high, high, w_win[...]))
    mine = own[...]
    for c in range(comps):
        s2.append(lanes(sw, -64 - 8 * c))
        s3.append(lanes(sw, -96 - 8 * c))
        w1.append(lanes(ww, -32 - 8 * c))
        w0.append(lanes(ww, -8 * c))
        own_s.append(lanes(mine, -64 - 8 * c))
        own_w.append(lanes(mine, -32 - 8 * c))

    for kind, layer, blend in ((0, s2, blend_rot), (1, w1, blend_sta)):
        for c in range(comps):
            g = blend(layer[c], f)
            here = rows(g, -1)
            ghost1[kind, 0, c] = spread(here, 0)
            ghost1[kind, 1, c] = spread(here, planes + 1)
            first = jnp.broadcast_to(g[0:1, :], (ROWS, LANE))
            after = jnp.broadcast_to(g[cells + 1 : cells + 2, :], (ROWS, LANE))
            picked = jnp.where(row8 < planes, first, after)
            picked = jnp.where(lane8 == row8 % planes + 1, picked, 0.0)
            ghost1[kind, 2, c] = jnp.broadcast_to(jnp.sum(picked, axis=1, keepdims=True), (ROWS, LANE))

    def far_section(q, up_r, dn_r):
        return advance(
            q,
            [lanes(x, -1) for x in q], [lanes(x, 1) for x in q],
            [rows(x, -1) for x in q], [rows(x, 1) for x in q],
            up_r, dn_r,
        )

    far_sta = [rows(blend_sta(x, f), -6)[: 2 * ROWS] for x in own_w]
    far_rot = [rows(blend_rot(x, f), -6)[: 2 * ROWS] for x in own_s]
    sec_s = far_section(s2, s3, far_sta)
    sec_w = far_section(w1, far_rot, w0)
    for kind, layer, blend in ((0, sec_s, blend_rot), (1, sec_w, blend_sta)):
        for c in range(comps):
            here = rows(blend(layer[c], f), -1)
            for p in range(planes):
                ghost2[kind, p, c] = spread(here, p + 1)

    row = iota((ROWS, CHUNK), 0)

    def build(k, carry):
        base = k * CHUNK
        at, padded = span(base, CHUNK), span(base + LANE, CHUNK)
        for c in range(comps):
            edge[c, :, padded] = jnp.where(row < planes, left[c, :, at], pltpu.roll(right[c, :, at], planes, 0))
            near[c, 0, :, padded] = choose(from_below, crossed, near_low, c, 1, at)
            near[c, 1, :, padded] = choose(from_above, crossed, near_high, c, 0, at)
        return carry

    lax.fori_loop(0, radial // CHUNK, build, 0)

    def first(k, carry):
        base = k * CHUNK
        at, padded = span(base, CHUNK), span(base + LANE, CHUNK)
        for s, late, outside in ((0, late_low, 0), (1, late_high, last)):
            q, up_p, dn_p, up_t, dn_t, up_r, dn_r = [], [], [], [], [], [], []
            for c in range(comps):
                x = near[c, s, :, padded]
                q.append(x)
                if s:
                    far = choose(from_above, crossed, near_high, c, 1, at)
                else:
                    far = choose(from_below, crossed, near_low, c, 0, at)
                up_p.append(far if s else st[c, 0, :, at])
                dn_p.append(st[c, planes - 1, :, at] if s else far)
                u, d = azimuthal_pair(x, late[2 * c : 2 * c + 1, at], late[2 * c + 1 : 2 * c + 2, at])
                up_t.append(u)
                dn_t.append(d)
                u, d = radial_pair(
                    lambda b, w: near[c, s, :, span(b, w)], ghost1[0, s, c], ghost1[1, s, c], base, inner
                )
                up_r.append(u)
                dn_r.append(d)
            new = advance(q, up_p, dn_p, up_t, dn_t, up_r, dn_r)
            for c in range(comps):
                near_sect[c, s, :, padded] = jnp.where(position == outside, 0.0, new[c])
        q, up_p, dn_p, up_t, dn_t, up_r, dn_r = [], [], [], [], [], [], []
        for c in range(comps):
            x = edge[c, :, padded]
            q.append(x)
            u, d = pltpu.roll(x, ROWS - 1, 0), pltpu.roll(x, 1, 0)
            u = jnp.where(row == planes - 1, late_high[2 * c : 2 * c + 1, at], u)
            u = jnp.where(row == 2 * planes - 1, late_high[2 * c + 1 : 2 * c + 2, at], u)
            d = jnp.where(row == 0, late_low[2 * c : 2 * c + 1, at], d)
            d = jnp.where(row == planes, late_low[2 * c + 1 : 2 * c + 2, at], d)
            up_p.append(u)
            dn_p.append(d)
            up_t.append(jnp.where(row < planes, dn_msg[c, :, at], right[c, :, at]))
            dn_t.append(pltpu.roll(jnp.where(row < planes, up_msg[c, :, at], left[c, :, at]), planes, 0))
            u, d = radial_pair(
                lambda b, w: edge[c, :, span(b, w)], ghost1[0, 2, c], ghost1[1, 2, c], base, inner
            )
            up_r.append(u)
            dn_r.append(d)
        new = advance(q, up_p, dn_p, up_t, dn_t, up_r, dn_r)
        for c in range(comps):
            edge_sect[c, :, at] = new[c]
        return carry

    lax.fori_loop(0, radial // CHUNK, first, 0)

    def second(k, carry):
        base = k * CHUNK
        at, padded = span(base, CHUNK), span(base + LANE, CHUNK)
        for p in range(planes):
            q, up_p, dn_p, up_t, dn_t, up_r, dn_r = [], [], [], [], [], [], []
            for c in range(comps):
                x = sect[c, p, :, padded]
                q.append(x)
                up_p.append(near_sect[c, 1, :, padded] if p == planes - 1 else sect[c, p + 1, :, padded])
                dn_p.append(near_sect[c, 0, :, padded] if p == 0 else sect[c, p - 1, :, padded])
                u, d = azimuthal_pair(x, edge_sect[c, p : p + 1, at], edge_sect[c, planes + p : planes + p + 1, at])
                up_t.append(u)
                dn_t.append(d)
                u, d = radial_pair(
                    lambda b, w: sect[c, p, :, span(b, w)], ghost2[0, p, c], ghost2[1, p, c], base, inner
                )
                up_r.append(u)
                dn_r.append(d)
            new = advance(q, up_p, dn_p, up_t, dn_t, up_r, dn_r)
            for c in range(comps):
                result[c, p, :, at] = 0.5 * (st[c, p, :, at] + new[c])
        pltpu.make_async_copy(result.at[:, :, :, at], out.at[:, :, :, at], sem).start()
        return carry

    lax.fori_loop(0, radial // CHUNK, second, 0)
    pltpu.make_async_copy(result, out, sem).wait()


def shards(state, rotor_offset, rotor_fraction):
    comps, planes, cells, radial = state.shape
    n_ax, n_az = lax.axis_size("ax"), lax.axis_size("az")
    position = lax.axis_index("ax")
    offset = rotor_offset[0]
    shift = (offset + cells // 2) // cells
    turn = offset - shift * cells
    where = jnp.stack([lax.axis_index("az"), shift, turn])
    half = n_ax // 2
    info = jnp.stack([position, jnp.int32(n_ax - 1), jnp.int32(half)])

    crossing = pl.pallas_call(
        cross_kernel,
        out_shape=shape(comps, 2, cells, radial),
        in_specs=[smem(), vmem()],
        out_specs=vmem(),
        compiler_params=params(16),
        name="pack_cross",
    )(info, state)
    crossed = lax.ppermute(crossing, "ax", [(half - 1, half), (half, half - 1)])
    up_msg, dn_msg, low, high, layers = pl.pallas_call(
        pack_kernel,
        out_shape=[shape(comps, cells, radial)] * 2 + [shape(comps, 2, cells, radial)] * 2 + [shape(ROWS, LANE)],
        in_specs=[vmem(), hbm()],
        out_specs=[vmem()] * 5,
        compiler_params=params(16),
        name="pack",
    )(state, crossing)
    onward = [(i, i + 1) for i in range(n_ax - 1)]
    backward = [(i + 1, i) for i in range(n_ax - 1)]
    from_prev = lax.ppermute(high, "ax", [pair for pair in onward if half - 1 not in pair or half not in pair])
    from_next = lax.ppermute(low, "ax", [pair for pair in backward if half - 1 not in pair or half not in pair])
    left = lax.ppermute(up_msg, "az", [(i, (i + 1) % n_az) for i in range(n_az)])
    right = lax.ppermute(dn_msg, "az", [((i + 1) % n_az, i) for i in range(n_az)])

    tiles = lax.all_to_all(jnp.broadcast_to(layers, (n_az, ROWS, LANE)), "az", 0, 0)
    to_next, to_prev, s_win, w_win, own = pl.pallas_call(
        window_kernel,
        out_shape=[shape(cells, radial + 2 * LANE)] * 2 + [shape(2 * cells, LANE)] * 2 + [shape(4 * cells, LANE)],
        in_specs=[smem()] + [vmem()] * 3,
        out_specs=[vmem()] * 5,
        compiler_params=params(16),
        name="pack_window",
    )(where, tiles, left, right)
    late_low = lax.ppermute(to_next, "ax", onward)
    late_high = lax.ppermute(to_prev, "ax", backward)

    wide = radial + 2 * LANE
    cells_all = planes * cells * radial
    sect = pl.pallas_call(
        own_kernel,
        out_shape=shape(comps, planes, cells, wide),
        in_specs=[smem(), smem()] + [vmem()] * 8,
        out_specs=vmem(),
        scratch_shapes=[
            pltpu.VMEM((comps, planes, cells, wide), f32),
            pltpu.VMEM((2, planes, comps, ROWS, LANE), f32),
        ],
        cost_estimate=pl.CostEstimate(flops=120 * cells_all, bytes_accessed=48 * cells_all, transcendentals=cells_all),
        compiler_params=params(16),
        name="own_section",
    )(info, rotor_fraction, state, crossed, from_prev, from_next, left, right, s_win, w_win)
    return pl.pallas_call(
        step_kernel,
        out_shape=shape(*state.shape),
        in_specs=[smem(), smem()] + [vmem()] * 14,
        out_specs=hbm(),
        scratch_shapes=[
            pltpu.VMEM((comps, 2, cells, wide), f32),
            pltpu.VMEM((comps, 2, cells, wide), f32),
            pltpu.VMEM((comps, 2 * planes, wide), f32),
            pltpu.VMEM((comps, 2 * planes, radial), f32),
            pltpu.VMEM((2, 3, comps, ROWS, LANE), f32),
            pltpu.VMEM((2, planes, comps, ROWS, LANE), f32),
            pltpu.VMEM(state.shape, f32),
            pltpu.SemaphoreType.DMA,
        ],
        compiler_params=params(24),
        name="step",
    )(
        info, rotor_fraction, state, crossed, from_prev, from_next, sect,
        left, right, up_msg, dn_msg, late_low, late_high, s_win, w_win, own,
    )


def solution(mesh):
    return jax.shard_map(
        shards,
        mesh=mesh,
        in_specs=(P(None, "ax", "az", None), P(), P()),
        out_specs=P(None, "ax", "az", None),
        check_vma=False,
    )
```
